32 devices in a mesh: dom: 8 (over z, x), slab: 4 (over y, core).
Axes of the slice: x: 2, y: 2, z: 4, core: 2. Of those that a mesh axis runs over, the one named last changes fastest.
Arguments:
- basis_weights: float32 [4, 4, 12288], P(None, 'slab', 'dom'), may hold values from 0 to 1, as said below
- velocity: float32 [3, 4, 12288], P(None, 'slab', 'dom'), may hold values from -6 to 6
- owner_dom: int32 [4, 12288, 1], P('slab', 'dom'), may hold values from 0 to 7; in each aligned block of 1536 rows (0 to 1535, 1536 to 3071, ..., all dimensions but the last counted through in order) at most 384 rows name the same one
- cell_local: int32 [4, 12288], P('slab', 'dom'), may hold values from 0 to 255
- inverse: float32 [16, 4, 2048], P(None, 'slab', 'dom'), may hold values from -0.2 to 1.5
- connectivity: int32 [4, 4, 2048], P(None, 'slab', 'dom'), may hold values from 0 to 2303, as said below
Outputs:
- coefficients: float32 [12, 4, 2048], P(None, 'slab', 'dom')
- node_values: float32 [3, 4, 2048], P(None, 'slab', 'dom')
The draws below stay inside these ranges and needn't reach their ends.
Inputs may be any that keep to these rules, and one draw needn't show every extreme that they name: `basis_weights`: the four entries of each particle are positive and sum to one. `owner_dom`: among the rows of one device, no owner is named more than 384 times. `connectivity`: the slab move and dom move are each -1, 0 or 1, and the node they name lies inside the domain.
All inputs are finite; a program needn't handle non-finite values.
Results may differ from the reference program's by a relative error of at most 0.00011.
Values sent between devices are 32-bit elements; how exact they have to be, the bound alone decides.
No kernel may reach another device: no remote copies, remote signals or barrier semaphores. Data moves between devices by JAX's collectives and lax.ppermute only.
A program may use at most 64 MiB of HBM per device.

```python
import math
import jax
import jax.numpy as jnp
import numpy as np
from jax import lax

P_DEV = 1536
CELLS_DEV = 256
NODES_DEV = 256
DOMS = 8
SLABS = 4
P_SLAB = 12288
CELLS_SLAB = 2048
NODES_SLAB = 2048
CAP = 384


def draw_basis_weights(key, part):
    shape = (4, SLABS, P_SLAB)
    uniform_draw = jax.random.uniform(key, shape, jnp.float32, 0.05, 1.0)
    return uniform_draw / jnp.sum(uniform_draw, axis=0, keepdims=True)


def draw_inverse(key, part):
    shape = (16, SLABS, CELLS_SLAB)
    first_key, second_key = jax.random.split(key)
    entry_row = lax.broadcasted_iota(jnp.int32, shape, 0)
    on_diagonal = entry_row % 5 == 0
    diagonal = jax.random.uniform(first_key, shape, jnp.float32, 0.3, 1.2)
    off_part = jax.random.uniform(second_key, shape, jnp.float32, -0.15, 0.15)
    return jnp.where(on_diagonal, diagonal, off_part)


def draw_connectivity(key, part):
    shape = (4, SLABS, CELLS_SLAB)
    first_key, second_key, third_key = jax.random.split(key, 3)
    slab_index = lax.broadcasted_iota(jnp.int32, shape, 1)
    cell_index = lax.broadcasted_iota(jnp.int32, shape, 2)
    home_dom = cell_index // CELLS_DEV
    slab_roll = jax.random.randint(first_key, shape, 0, 8)
    dom_roll = jax.random.randint(second_key, shape, 0, 8)
    slab_move = jnp.where(slab_roll == 0, -1, jnp.where(slab_roll == 1, 1, 0))
    dom_move = jnp.where(dom_roll == 0, -1, jnp.where(dom_roll == 1, 1, 0))
    node_slab = jnp.clip(slab_index + slab_move, 0, SLABS - 1)
    node_dom = jnp.clip(home_dom + dom_move, 0, DOMS - 1)
    local_node = jax.random.randint(third_key, shape, 0, NODES_DEV)
    relative = ((node_slab - slab_index + 1) * 3 + node_dom - home_dom + 1) * NODES_DEV + local_node
    return relative.astype(jnp.int32)


def with_ends(entries, stream_key, smallest, largest):
    extent = entries.shape
    place = [jax.random.randint(jax.random.fold_in(stream_key, axis), (), 0, extent[axis]) for axis in range(len(extent))]
    entries = entries.at[tuple(place)].set(smallest)
    longest = extent.index(max(extent))
    place[longest] = (place[longest] + 1) % extent[longest]
    return entries.at[tuple(place)].set(largest)


def levels(rng, dims, pieces, low, largest):
    gain = 1.0
    for axis_at, blocks in pieces:
        draws = jax.random.uniform(jax.random.fold_in(jax.random.fold_in(rng, 6), axis_at), (blocks,), jnp.float32, low / len(pieces), largest / len(pieces))
        gain = gain * jnp.repeat(jnp.exp(draws), dims[axis_at] // blocks).reshape((-1,) + (1,) * (len(dims) - 1 - axis_at))
    return gain


def deal_out(own_key, own, number, rows, amount, top, bound, skew):
    sequence = jax.random.permutation(own_key, amount)
    packed, common = portions_of(amount, rows * top, bound, skew, True), portions_of(amount, rows * top, bound, skew, False)
    places = jnp.arange(amount)

    def named(tallies, offset_by):
        used = int((tallies > 0).sum())
        fixed = max(1, used // 4)
        shifted = fixed + (places - fixed + offset_by * (used - fixed)) % max(1, amount - fixed)
        return jnp.zeros((amount,), jnp.int32).at[sequence[jnp.where(places < fixed, places, shifted)]].set(jnp.asarray(tallies, jnp.int32))

    tallies = jnp.where(number % 4 == 0, named(packed, number // 4), named(common, number - number // 4 - 1))
    mixed = jax.random.permutation(jax.random.fold_in(own, 3), amount)
    giver, sink = mixed[0:amount // 2 * 2:2], mixed[1:amount // 2 * 2:2]
    room = jnp.minimum(tallies[giver] - 1, bound - tallies[sink]) // 2
    room = jnp.where((giver == sequence[0]) | (sink == sequence[0]) | (tallies[sink] == 0), 0, jnp.maximum(room, 0))
    shifted = jax.random.randint(jax.random.fold_in(own, 4), (amount // 2,), 0, 1 << 20) % (room + 1)
    tallies = tallies.at[giver].add(-shifted).at[sink].add(shifted)
    members = jnp.searchsorted(jnp.cumsum(tallies), jnp.arange(rows * top), side="right").astype(jnp.int32)
    grid = members.reshape(top, rows).T
    grid = grid[jax.random.permutation(jax.random.fold_in(own, 1), rows)]
    offset_by = jax.random.randint(jax.random.fold_in(own, 2), (rows, 1), 0, top)
    return jnp.take_along_axis(grid, (jnp.arange(top)[None, :] + offset_by) % top, axis=1)


def portions_of(count, total, reach, skew, full):
    loads = [(1 << 20) // math.isqrt(rank ** skew) + 1 for rank in range(1, count + 1)]
    largest = reach if full else min(reach, max(-(-total // count), total * loads[0] // sum(loads)))
    least = 1 if total - largest >= count - 1 else 0
    given, rest = [largest] + [least] * (count - 1), total - largest - least * (count - 1)
    while rest > 0:
        candidates = [i for i in range(1, count) if given[i] < largest] or [i for i in range(1, count) if given[i] < reach]
        pool, budget = sum([loads[i] for i in candidates]), rest
        for i in candidates:
            extra = min(reach - given[i], max(1, budget * loads[i] // pool), rest)
            given[i] = given[i] + extra
            rest = rest - extra
    return np.array(given)


def normal_values(key, dims, deviation, bound, shards=(), held_as=jnp.bfloat16):
    entries = jax.random.normal(key, dims, jnp.float32) * deviation
    if len(shards) > 0:
        entries = levels(key, dims, shards, -0.22, 0.18) * entries
    return jnp.clip(entries, min=-bound, max=bound).astype(held_as)


def setup_inputs(seed: int = 0) -> dict:
    keys = jax.random.split(jax.random.key(seed), 7)
    basis_weights = draw_basis_weights(jax.random.fold_in(keys[6], 71), 0)
    velocity = normal_values(keys[1], (3, SLABS, P_SLAB), 1.0, 6.0, ((1, 4), (2, 8)), jnp.float32)
    owner_dom_keys = jax.random.split(jax.random.fold_in(keys[2], 1), SLABS * P_SLAB // P_DEV)
    owner_dom_turns = jax.random.permutation(jax.random.fold_in(keys[2], 3), SLABS * P_SLAB // P_DEV)
    owner_dom = jax.vmap(lambda own, number: deal_out(jax.random.fold_in(keys[2], 2), own, number, P_DEV, DOMS, 1, CAP, 1))(owner_dom_keys, owner_dom_turns).reshape((SLABS, P_SLAB, 1))
    cell_local = with_ends(jax.random.randint(keys[3], (SLABS, P_SLAB), 0, CELLS_DEV), jax.random.fold_in(keys[3], 1), 0, CELLS_DEV - 1).astype(jnp.int32)
    inverse = draw_inverse(jax.random.fold_in(keys[6], 71), 0)
    connectivity = draw_connectivity(jax.random.fold_in(keys[6], 71), 0)
    return dict(basis_weights=basis_weights, velocity=velocity, owner_dom=owner_dom, cell_local=cell_local, inverse=inverse, connectivity=connectivity)


def reference(basis_weights, velocity, owner_dom, cell_local, inverse, connectivity):
    def one_slab(slab_items):
        weights, velocities, owners, local_cells = slab_items
        target = owners[:, 0] * CELLS_DEV + local_cells
        gram_terms = (weights[:, None, :] * weights[None, :, :]).reshape(16, -1)
        moment_terms = (weights[:, None, :] * velocities[None, :, :]).reshape(12, -1)
        all_terms = jnp.concatenate([gram_terms, moment_terms], axis=0)
        return jax.ops.segment_sum(all_terms.T, target, num_segments=CELLS_SLAB).T

    totals = lax.map(one_slab, (jnp.moveaxis(basis_weights, 1, 0), jnp.moveaxis(velocity, 1, 0), owner_dom, cell_local))
    gram_full = totals[:, :16].reshape(SLABS, 4, 4, CELLS_SLAB)
    moment = totals[:, 16:].reshape(SLABS, 4, 3, CELLS_SLAB)
    matrix = jnp.moveaxis(inverse.reshape(4, 4, SLABS, CELLS_SLAB), 2, 0)
    highest = lax.Precision.HIGHEST
    first_pass = jnp.einsum("sijc,sjac->siac", matrix, moment, precision=highest)
    residual_part = moment - jnp.einsum("sjkc,skac->sjac", gram_full, first_pass, precision=highest)
    solved = first_pass + jnp.einsum("sijc,sjac->siac", matrix, residual_part, precision=highest)
    coefficients = jnp.moveaxis(solved.reshape(SLABS, 12, CELLS_SLAB), 0, 1)
    corner_values = jnp.transpose(solved, (1, 0, 3, 2)).reshape(-1, 3)
    shape = (4, SLABS, CELLS_SLAB)
    slab_index = lax.broadcasted_iota(jnp.int32, shape, 1)
    home_dom = lax.broadcasted_iota(jnp.int32, shape, 2) // CELLS_DEV
    node_slab = slab_index + connectivity // (3 * NODES_DEV) - 1
    node_dom = home_dom + (connectivity // NODES_DEV) % 3 - 1
    global_node = (node_slab * NODES_SLAB + node_dom * NODES_DEV + connectivity % NODES_DEV).astype(jnp.int32)
    assembled = jax.ops.segment_sum(corner_values, global_node.reshape(-1), num_segments=SLABS * NODES_SLAB)
    node_values = assembled.T.reshape(3, SLABS, NODES_SLAB)
    return coefficients, node_values
```

```python
import jax
import jax.numpy as jnp
from jax import lax
from jax.experimental import pallas as pl
from jax.experimental.pallas import tpu as pltpu
from jax.sharding import PartitionSpec as P

DOM_BLOCK = 8
TERMS = 24
NT = (((1,), (1,)), ((), ()))


def split_rows(values):
    high = values.astype(jnp.bfloat16)
    low = (values - high.astype(jnp.float32)).astype(jnp.bfloat16)
    return high, low


def one_hot_rows(index_row, count):
    rows = lax.broadcasted_iota(jnp.int32, (count, index_row.shape[1]), 0)
    return jnp.where(rows == index_row, 1.0, 0.0).astype(jnp.bfloat16)


def partial_sums_kernel(weights_ref, velocity_ref, owner_ref, cell_ref, sums_ref):
    cell_count = sums_ref.shape[2]
    first_dom = pl.program_id(0) * DOM_BLOCK
    w = weights_ref[:, 0, :]
    v = velocity_ref[:, 0, :]
    particles = w.shape[1]
    wide = (4, particles)
    turned = jnp.concatenate([w[1:], w[:1]], axis=0)
    across = jnp.concatenate([w[2:], w[:2]], axis=0)
    terms = jnp.concatenate(
        [
            w * w,
            w * turned,
            w * across,
            w * jnp.broadcast_to(v[0:1], wide),
            w * jnp.broadcast_to(v[1:2], wide),
            w * jnp.broadcast_to(v[2:3], wide),
        ],
        axis=0,
    )
    high, low = split_rows(terms)
    both = jnp.concatenate([high, low], axis=0)
    owner = owner_ref[...]
    picked = []
    for d in range(DOM_BLOCK):
        named = jnp.where(owner == first_dom + d, 1.0, 0.0).astype(jnp.bfloat16)
        picked.append(both * named)
    left = jnp.concatenate(picked, axis=0)
    right = one_hot_rows(cell_ref[...], cell_count)
    sums = lax.dot_general(left, right, NT, preferred_element_type=jnp.float32)
    for d in range(DOM_BLOCK):
        at = 2 * TERMS * d
        sums_ref[d] = sums[at : at + TERMS] + sums[at + TERMS : at + 2 * TERMS]


def partial_sums(basis_weights, velocity, owner, cell_local, dom_count, cell_count):
    particles = cell_local.shape[1]
    full = lambda shape: pl.BlockSpec(shape, lambda i: (0,) * len(shape))
    return pl.pallas_call(
        partial_sums_kernel,
        grid=(dom_count // DOM_BLOCK,),
        in_specs=[
            full((4, 1, particles)),
            full((3, 1, particles)),
            full((1, particles)),
            full((1, particles)),
        ],
        out_specs=pl.BlockSpec((DOM_BLOCK, TERMS, cell_count), lambda i: (i, 0, 0)),
        out_shape=jax.ShapeDtypeStruct((dom_count, TERMS, cell_count), jnp.float32),
        compiler_params=pltpu.CompilerParams(vmem_limit_bytes=48 * 1024 * 1024),
        name="partial_sums",
    )(basis_weights, velocity, owner, cell_local)


def solve_kernel(arrived_ref, inverse_ref, connectivity_ref, coefficients_ref, nodes_ref):
    cells = arrived_ref.shape[2]
    nodes = nodes_ref.shape[2]
    total = arrived_ref[0]
    for d in range(1, arrived_ref.shape[0]):
        total = total + arrived_ref[d]

    def gram(i, j):
        if i == j:
            row = i
        elif (j - i) % 4 == 1:
            row = 4 + i
        elif (i - j) % 4 == 1:
            row = 4 + j
        else:
            row = 8 + i
        return total[row : row + 1]

    wide = (4, cells)
    inverse_columns = [
        jnp.concatenate([inverse_ref[4 * i + j] for i in range(4)], axis=0) for j in range(4)
    ]
    gram_columns = [jnp.concatenate([gram(i, j) for i in range(4)], axis=0) for j in range(4)]
    solved = []
    for a in range(3):
        moment = total[12 + 4 * a : 16 + 4 * a]

        def apply(columns, vector):
            parts = [columns[j] * jnp.broadcast_to(vector[j : j + 1], wide) for j in range(4)]
            return (parts[0] + parts[1]) + (parts[2] + parts[3])

        first = apply(inverse_columns, moment)
        residual = moment - apply(gram_columns, first)
        solved.append(first + apply(inverse_columns, residual))
    for i in range(4):
        for a in range(3):
            coefficients_ref[3 * i + a] = solved[a][i : i + 1]
    left, right = [], []
    for k in range(4):
        values = jnp.concatenate(
            [solved[a][k : k + 1] for a in range(3)] + [jnp.zeros((1, cells), jnp.float32)], axis=0
        )
        values = jnp.concatenate([values, values], axis=0)
        entry = connectivity_ref[k]
        move = entry // nodes
        node = entry - move * nodes
        columns = []
        for m in range(0, 10, 2):
            rows = lax.broadcasted_iota(jnp.int32, (8, cells), 0) // 4 + m
            columns.append(jnp.where(rows == move, values, 0.0))
        left.append(jnp.concatenate(columns, axis=0))
        right.append(one_hot_rows(node, nodes))
    left = jnp.concatenate(left, axis=1)
    right = jnp.concatenate(right, axis=1)
    high, low = split_rows(left)
    both = jnp.concatenate([high, low], axis=0)
    sums = lax.dot_general(both, right, NT, preferred_element_type=jnp.float32)
    sums = sums[:40] + sums[40:]
    for m in range(9):
        nodes_ref[m] = sums[4 * m : 4 * m + 3]


def solve(arrived, inverse, connectivity, node_count):
    cells = arrived.shape[2]
    return pl.pallas_call(
        solve_kernel,
        out_shape=(
            jax.ShapeDtypeStruct((12, 1, cells), jnp.float32),
            jax.ShapeDtypeStruct((9, 3, node_count), jnp.float32),
        ),
        compiler_params=pltpu.CompilerParams(vmem_limit_bytes=48 * 1024 * 1024),
        name="solve",
    )(arrived, inverse, connectivity)


def shifted(array, axis, by):
    devices = lax.axis_size(axis)
    pairs = [(i, i + by) for i in range(devices) if 0 <= i + by < devices]
    return lax.ppermute(array, axis, pairs)


def per_device(basis_weights, velocity, owner_dom, cell_local, inverse, connectivity):
    particles = cell_local.shape[1]
    cells = inverse.shape[2]
    nodes = 256
    doms = lax.axis_size("dom")
    owner = owner_dom.reshape(1, particles)
    sums = partial_sums(basis_weights, velocity, owner, cell_local, doms, cells)
    arrived = lax.all_to_all(sums, "dom", split_axis=0, concat_axis=0, tiled=True)
    coefficients, local = solve(arrived, inverse, connectivity, nodes)
    local = local.reshape(3, 3, 3, nodes)
    merged = local[:, 1] + shifted(local[:, 2], "dom", 1) + shifted(local[:, 0], "dom", -1)
    total = merged[1] + shifted(merged[2], "slab", 1) + shifted(merged[0], "slab", -1)
    return coefficients, total.reshape(3, 1, nodes)


def solution(mesh):
    in_specs = (
        P(None, "slab", "dom"),
        P(None, "slab", "dom"),
        P("slab", "dom", None),
        P("slab", "dom"),
        P(None, "slab", "dom"),
        P(None, "slab", "dom"),
    )
    out_specs = (P(None, "slab", "dom"), P(None, "slab", "dom"))
    return jax.shard_map(
        per_device, mesh=mesh, in_specs=in_specs, out_specs=out_specs, check_vma=False
    )
```

```python
import jax
import jax.numpy as jnp
from jax import lax
from jax.experimental import pallas as pl
from jax.experimental.pallas import tpu as pltpu
from jax.sharding import PartitionSpec as P

DOM_BLOCK = 8
TERMS = 24
NT = (((1,), (1,)), ((), ()))


def split_rows(values):
    high = values.astype(jnp.bfloat16)
    low = (values - high.astype(jnp.float32)).astype(jnp.bfloat16)
    return high, low


def one_hot_rows(index_row, count):
    rows = lax.broadcasted_iota(jnp.int32, (count, index_row.shape[1]), 0)
    return jnp.where(rows == index_row, 1.0, 0.0).astype(jnp.bfloat16)


def partial_sums_kernel(
    weights_hbm, velocity_hbm, owner_hbm, cell_hbm, sums_ref,
    weights_ref, velocity_ref, owner_ref, cell_ref, arrivals,
):
    pairs = (
        (weights_hbm, weights_ref),
        (velocity_hbm, velocity_ref),
        (owner_hbm, owner_ref),
        (cell_hbm, cell_ref),
    )

    @pl.when(pl.program_id(0) == 0)
    def _():
        copies = [
            pltpu.make_async_copy(source, target, arrivals.at[i])
            for i, (source, target) in enumerate(pairs)
        ]
        for copy in copies:
            copy.start()
        for copy in copies:
            copy.wait()

    cell_count = sums_ref.shape[2]
    first_dom = pl.program_id(0) * DOM_BLOCK
    w = weights_ref[:, 0, :]
    v = velocity_ref[:, 0, :]
    particles = w.shape[1]
    wide = (4, particles)
    turned = jnp.concatenate([w[1:], w[:1]], axis=0)
    across = jnp.concatenate([w[2:], w[:2]], axis=0)
    terms = jnp.concatenate(
        [
            w * w,
            w * turned,
            w * across,
            w * jnp.broadcast_to(v[0:1], wide),
            w * jnp.broadcast_to(v[1:2], wide),
            w * jnp.broadcast_to(v[2:3], wide),
        ],
        axis=0,
    )
    high, low = split_rows(terms)
    both = jnp.concatenate([high, low], axis=0)
    owner = owner_ref[...]
    picked = []
    for d in range(DOM_BLOCK):
        named = jnp.where(owner == first_dom + d, 1.0, 0.0).astype(jnp.bfloat16)
        picked.append(both * named)
    left = jnp.concatenate(picked, axis=0)
    right = one_hot_rows(cell_ref[...], cell_count)
    sums = lax.dot_general(left, right, NT, preferred_element_type=jnp.float32)
    for d in range(DOM_BLOCK):
        at = 2 * TERMS * d
        sums_ref[d] = sums[at : at + TERMS] + sums[at + TERMS : at + 2 * TERMS]


def partial_sums(basis_weights, velocity, owner, cell_local, dom_count, cell_count):
    particles = cell_local.shape[1]
    return pl.pallas_call(
        partial_sums_kernel,
        grid=(dom_count // DOM_BLOCK,),
        in_specs=[pl.BlockSpec(memory_space=pltpu.HBM)] * 4,
        out_specs=pl.BlockSpec((DOM_BLOCK, TERMS, cell_count), lambda i: (i, 0, 0)),
        out_shape=jax.ShapeDtypeStruct((dom_count, TERMS, cell_count), jnp.float32),
        scratch_shapes=[
            pltpu.VMEM((4, 1, particles), jnp.float32),
            pltpu.VMEM((3, 1, particles), jnp.float32),
            pltpu.VMEM((1, particles), jnp.int32),
            pltpu.VMEM((1, particles), jnp.int32),
            pltpu.SemaphoreType.DMA((4,)),
        ],
        compiler_params=pltpu.CompilerParams(vmem_limit_bytes=48 * 1024 * 1024),
        name="partial_sums",
    )(*(pltpu.with_memory_space_constraint(a, pltpu.HBM) for a in (basis_weights, velocity, owner, cell_local)))


def solve_kernel(
    arrived_ref, inverse_ref, connectivity_ref,
    coefficients_ref, dom_far_ref, dom_near_ref, own_ref,
):
    cells = arrived_ref.shape[2]
    nodes = own_ref.shape[2]
    dom_odd = lax.rem(lax.axis_index("dom"), 2)
    slab_odd = lax.rem(lax.axis_index("slab"), 2)
    dom_moves = (2 * dom_odd, 2 - 2 * dom_odd, 1)
    slab_moves = (2 * slab_odd, 2 - 2 * slab_odd, 1)
    wanted = [3 * slab_move + dom_move for dom_move in dom_moves for slab_move in slab_moves]
    total = arrived_ref[0]
    for d in range(1, arrived_ref.shape[0]):
        total = total + arrived_ref[d]

    def gram(i, j):
        if i == j:
            row = i
        elif (j - i) % 4 == 1:
            row = 4 + i
        elif (i - j) % 4 == 1:
            row = 4 + j
        else:
            row = 8 + i
        return total[row : row + 1]

    wide = (4, cells)
    inverse_columns = [
        jnp.concatenate([inverse_ref[4 * i + j] for i in range(4)], axis=0) for j in range(4)
    ]
    gram_columns = [jnp.concatenate([gram(i, j) for i in range(4)], axis=0) for j in range(4)]
    solved = []
    for a in range(3):
        moment = total[12 + 4 * a : 16 + 4 * a]

        def apply(columns, vector):
            parts = [columns[j] * jnp.broadcast_to(vector[j : j + 1], wide) for j in range(4)]
            return (parts[0] + parts[1]) + (parts[2] + parts[3])

        first = apply(inverse_columns, moment)
        residual = moment - apply(gram_columns, first)
        solved.append(first + apply(inverse_columns, residual))
    for i in range(4):
        for a in range(3):
            coefficients_ref[3 * i + a] = solved[a][i : i + 1]
    left, right = [], []
    for k in range(4):
        values = jnp.concatenate(
            [solved[a][k : k + 1] for a in range(3)] + [jnp.zeros((1, cells), jnp.float32)], axis=0
        )
        values = jnp.concatenate([values, values], axis=0)
        entry = connectivity_ref[k]
        move = entry // nodes
        node = entry - move * nodes
        columns = []
        upper = lax.broadcasted_iota(jnp.int32, (8, cells), 0) < 4
        for m in range(0, 10, 2):
            rows = jnp.where(upper, wanted[m], wanted[m + 1] if m < 8 else -1)
            columns.append(jnp.where(rows == move, values, 0.0))
        left.append(jnp.concatenate(columns, axis=0))
        right.append(one_hot_rows(node, nodes))
    left = jnp.concatenate(left, axis=1)
    right = jnp.concatenate(right, axis=1)
    high, low = split_rows(left)
    both = jnp.concatenate([high, low], axis=0)
    sums = lax.dot_general(both, right, NT, preferred_element_type=jnp.float32)
    sums = sums[:40] + sums[40:]
    for m in range(9):
        (dom_far_ref, dom_near_ref, own_ref)[m // 3][m % 3] = sums[4 * m : 4 * m + 4]


def solve(arrived, inverse, connectivity, node_count):
    cells = arrived.shape[2]
    return pl.pallas_call(
        solve_kernel,
        out_shape=(
            jax.ShapeDtypeStruct((12, 1, cells), jnp.float32),
        )
        + (jax.ShapeDtypeStruct((3, 4, node_count), jnp.float32),) * 3,
        compiler_params=pltpu.CompilerParams(vmem_limit_bytes=48 * 1024 * 1024),
        name="solve",
    )(arrived, inverse, connectivity)


def swap_near(array, axis):
    devices = lax.axis_size(axis)
    return lax.ppermute(array, axis, [(i, i ^ 1) for i in range(devices)])


def swap_far(array, axis, close):
    devices = lax.axis_size(axis)
    pairs = [(i, ((i + 1) ^ 1) - 1) for i in range(1, devices - 1)]
    if close:
        pairs = [(0, devices - 1)] + pairs + [(devices - 1, 0)]
    return lax.ppermute(array, axis, pairs)


def per_device(basis_weights, velocity, owner_dom, cell_local, inverse, connectivity):
    particles = cell_local.shape[1]
    cells = inverse.shape[2]
    nodes = 256
    doms = lax.axis_size("dom")
    owner = owner_dom.reshape(1, particles)
    sums = partial_sums(basis_weights, velocity, owner, cell_local, doms, cells)
    arrived = lax.all_to_all(sums, "dom", split_axis=0, concat_axis=0, tiled=True)
    coefficients, dom_far, dom_near, own = solve(arrived, inverse, connectivity, nodes)
    merged = own + swap_far(dom_far, "dom", False) + swap_near(dom_near, "dom")
    total = merged[2] + swap_far(merged[0], "slab", True) + swap_near(merged[1], "slab")
    return coefficients, total[:3].reshape(3, 1, nodes)


def solution(mesh):
    in_specs = (
        P(None, "slab", "dom"),
        P(None, "slab", "dom"),
        P("slab", "dom", None),
        P("slab", "dom"),
        P(None, "slab", "dom"),
        P(None, "slab", "dom"),
    )
    out_specs = (P(None, "slab", "dom"), P(None, "slab", "dom"))
    return jax.shard_map(
        per_device, mesh=mesh, in_specs=in_specs, out_specs=out_specs, check_vma=False
    )
```

```python
import jax
import jax.numpy as jnp
from jax import lax
from jax.experimental import pallas as pl
from jax.experimental.pallas import tpu as pltpu
from jax.sharding import PartitionSpec as P

DOM_BLOCK = 8
TERMS = 24
NT = (((1,), (1,)), ((), ()))


def split_rows(values):
    high = values.astype(jnp.bfloat16)
    low = (values - high.astype(jnp.float32)).astype(jnp.bfloat16)
    return high, low


def one_hot_rows(index_row, count):
    rows = lax.broadcasted_iota(jnp.int32, (count, index_row.shape[1]), 0)
    return jnp.where(rows == index_row, 1.0, 0.0).astype(jnp.bfloat16)


def partial_sums_kernel(
    weights_hbm, velocity_hbm, owner_hbm, cell_hbm, sums_ref,
    weights_ref, velocity_ref, owner_ref, cell_ref, arrivals,
):
    pairs = (
        (weights_hbm, weights_ref),
        (velocity_hbm, velocity_ref),
        (owner_hbm, owner_ref),
        (cell_hbm, cell_ref),
    )

    @pl.when(pl.program_id(0) == 0)
    def _():
        copies = [
            pltpu.make_async_copy(source, target, arrivals.at[i])
            for i, (source, target) in enumerate(pairs)
        ]
        for copy in copies:
            copy.start()
        for copy in copies:
            copy.wait()

    cell_count = sums_ref.shape[2]
    first_dom = pl.program_id(0) * DOM_BLOCK
    w = weights_ref[:, 0, :]
    v = velocity_ref[:, 0, :]
    particles = w.shape[1]
    wide = (4, particles)
    turned = jnp.concatenate([w[1:], w[:1]], axis=0)
    across = jnp.concatenate([w[2:], w[:2]], axis=0)
    terms = jnp.concatenate(
        [
            w * w,
            w * turned,
            w * across,
            w * jnp.broadcast_to(v[0:1], wide),
            w * jnp.broadcast_to(v[1:2], wide),
            w * jnp.broadcast_to(v[2:3], wide),
        ],
        axis=0,
    )
    high, low = split_rows(terms)
    both = jnp.concatenate([high, low], axis=0)
    owner = owner_ref[...]
    picked = []
    for d in range(DOM_BLOCK):
        named = jnp.where(owner == first_dom + d, 1.0, 0.0).astype(jnp.bfloat16)
        picked.append(both * named)
    left = jnp.concatenate(picked, axis=0)
    right = one_hot_rows(cell_ref[...], cell_count)
    sums = lax.dot_general(left, right, NT, preferred_element_type=jnp.float32)
    for d in range(DOM_BLOCK):
        at = 2 * TERMS * d
        sums_ref[d] = sums[at : at + TERMS] + sums[at + TERMS : at + 2 * TERMS]


def partial_sums(basis_weights, velocity, owner, cell_local, dom_count, cell_count):
    particles = cell_local.shape[1]
    return pl.pallas_call(
        partial_sums_kernel,
        grid=(dom_count // DOM_BLOCK,),
        in_specs=[pl.BlockSpec(memory_space=pltpu.HBM)] * 4,
        out_specs=pl.BlockSpec((DOM_BLOCK, TERMS, cell_count), lambda i: (i, 0, 0)),
        out_shape=jax.ShapeDtypeStruct((dom_count, TERMS, cell_count), jnp.float32),
        scratch_shapes=[
            pltpu.VMEM((4, 1, particles), jnp.float32),
            pltpu.VMEM((3, 1, particles), jnp.float32),
            pltpu.VMEM((1, particles), jnp.int32),
            pltpu.VMEM((1, particles), jnp.int32),
            pltpu.SemaphoreType.DMA((4,)),
        ],
        compiler_params=pltpu.CompilerParams(vmem_limit_bytes=48 * 1024 * 1024),
        name="partial_sums",
    )(*(pltpu.with_memory_space_constraint(a, pltpu.HBM) for a in (basis_weights, velocity, owner, cell_local)))


def solve_kernel(
    arrived_ref, inverse_ref, connectivity_ref,
    coefficients_ref, dom_far_ref, dom_near_ref, own_ref,
):
    cells = arrived_ref.shape[2]
    nodes = own_ref.shape[2]
    dom_odd = lax.rem(lax.axis_index("dom"), 2)
    slab_odd = lax.rem(lax.axis_index("slab"), 2)
    dom_moves = (2 * dom_odd, 2 - 2 * dom_odd, 1)
    slab_moves = (2 * slab_odd, 2 - 2 * slab_odd, 1)
    wanted = [3 * slab_move + dom_move for dom_move in dom_moves for slab_move in slab_moves]
    total = arrived_ref[0]
    for d in range(1, arrived_ref.shape[0]):
        total = total + arrived_ref[d]

    def gram(i, j):
        if i == j:
            row = i
        elif (j - i) % 4 == 1:
            row = 4 + i
        elif (i - j) % 4 == 1:
            row = 4 + j
        else:
            row = 8 + i
        return total[row : row + 1]

    wide = (4, cells)
    inverse_columns = [
        jnp.concatenate([inverse_ref[4 * i + j] for i in range(4)], axis=0) for j in range(4)
    ]
    gram_columns = [jnp.concatenate([gram(i, j) for i in range(4)], axis=0) for j in range(4)]
    solved = []
    for a in range(3):
        moment = total[12 + 4 * a : 16 + 4 * a]

        def apply(columns, vector):
            parts = [columns[j] * jnp.broadcast_to(vector[j : j + 1], wide) for j in range(4)]
            return (parts[0] + parts[1]) + (parts[2] + parts[3])

        first = apply(inverse_columns, moment)
        residual = moment - apply(gram_columns, first)
        solved.append(first + apply(inverse_columns, residual))
    for i in range(4):
        for a in range(3):
            coefficients_ref[3 * i + a] = solved[a][i : i + 1]
    left, right = [], []
    for k in range(4):
        values = jnp.concatenate(
            [solved[a][k : k + 1] for a in range(3)] + [jnp.zeros((1, cells), jnp.float32)], axis=0
        )
        values = jnp.concatenate([values, values], axis=0)
        entry = connectivity_ref[k]
        move = entry // nodes
        node = entry - move * nodes
        columns = []
        upper = lax.broadcasted_iota(jnp.int32, (8, cells), 0) < 4
        for m in range(0, 10, 2):
            rows = jnp.where(upper, wanted[m], wanted[m + 1] if m < 8 else -1)
            columns.append(jnp.where(rows == move, values, 0.0))
        left.append(jnp.concatenate(columns, axis=0))
        right.append(one_hot_rows(node, nodes))
    left = jnp.concatenate(left, axis=1)
    right = jnp.concatenate(right, axis=1)
    high, low = split_rows(left)
    both = jnp.concatenate([high, low], axis=0)
    sums = lax.dot_general(both, right, NT, preferred_element_type=jnp.float32)
    sums = sums[:40] + sums[40:]
    for m in range(9):
        (dom_far_ref, dom_near_ref, own_ref)[m // 3][m % 3] = sums[4 * m : 4 * m + 4]


def solve(arrived, inverse, connectivity, node_count):
    cells = arrived.shape[2]
    return pl.pallas_call(
        solve_kernel,
        out_shape=(
            jax.ShapeDtypeStruct((12, 1, cells), jnp.float32),
        )
        + (jax.ShapeDtypeStruct((3, 4, node_count), jnp.float32),) * 3,
        compiler_params=pltpu.CompilerParams(vmem_limit_bytes=48 * 1024 * 1024),
        name="solve",
    )(arrived, inverse, connectivity)


def swap_near(array, axis):
    devices = lax.axis_size(axis)
    return lax.ppermute(array, axis, [(i, i ^ 1) for i in range(devices)])


def swap_far_slab(array):
    slabs = lax.axis_size("slab")
    pairs = [(i, ((i + 1) ^ 1) - 1) for i in range(1, slabs - 1)]
    return lax.ppermute(array, "slab", [(0, slabs - 1)] + pairs + [(slabs - 1, 0)])


def swap_far_dom(array):
    doms, slabs = lax.axis_size("dom"), lax.axis_size("slab")
    pairs = []
    for d in range(doms):
        for s in range(slabs):
            inside = 0 < d < doms - 1
            to = (((d + 1) ^ 1) - 1) * slabs + s if inside else d * slabs + (s ^ 1)
            pairs.append((d * slabs + s, to))
    return lax.ppermute(array, ("dom", "slab"), pairs)


def per_device(basis_weights, velocity, owner_dom, cell_local, inverse, connectivity):
    particles = cell_local.shape[1]
    cells = inverse.shape[2]
    nodes = 256
    doms = lax.axis_size("dom")
    owner = owner_dom.reshape(1, particles)
    sums = partial_sums(basis_weights, velocity, owner, cell_local, doms, cells)
    arrived = lax.all_to_all(sums, "dom", split_axis=0, concat_axis=0, tiled=True)
    coefficients, dom_far, dom_near, own = solve(arrived, inverse, connectivity, nodes)
    merged = own + swap_far_dom(dom_far) + swap_near(dom_near, "dom")
    total = merged[2] + swap_far_slab(merged[0]) + swap_near(merged[1], "slab")
    return coefficients, total[:3].reshape(3, 1, nodes)


def solution(mesh):
    in_specs = (
        P(None, "slab", "dom"),
        P(None, "slab", "dom"),
        P("slab", "dom", None),
        P("slab", "dom"),
        P(None, "slab", "dom"),
        P(None, "slab", "dom"),
    )
    out_specs = (P(None, "slab", "dom"), P(None, "slab", "dom"))
    return jax.shard_map(
        per_device, mesh=mesh, in_specs=in_specs, out_specs=out_specs, check_vma=False
    )
```

```python
import jax
import jax.numpy as jnp
from jax import lax
from jax.experimental import pallas as pl
from jax.experimental.pallas import tpu as pltpu
from jax.sharding import PartitionSpec as P

DOM_BLOCK = 8
TERMS = 24
NT = (((1,), (1,)), ((), ()))


def split_rows(values):
    high = values.astype(jnp.bfloat16)
    low = (values - high.astype(jnp.float32)).astype(jnp.bfloat16)
    return high, low


def one_hot_rows(index_row, count):
    lanes = 128
    rows = lax.broadcasted_iota(jnp.int32, (count, lanes), 0).astype(jnp.bfloat16)
    index = index_row.astype(jnp.float32).astype(jnp.bfloat16)
    one, zero = jnp.bfloat16(1), jnp.bfloat16(0)
    return jnp.concatenate(
        [
            jnp.where(rows == index[:, at : at + lanes], one, zero)
            for at in range(0, index_row.shape[1], lanes)
        ],
        axis=1,
    )


def partial_sums_kernel(
    weights_hbm, velocity_hbm, owner_hbm, cell_hbm, sums_ref,
    weights_ref, velocity_ref, owner_ref, cell_ref, arrivals,
):
    pairs = (
        (weights_hbm, weights_ref),
        (velocity_hbm, velocity_ref),
        (owner_hbm, owner_ref),
        (cell_hbm, cell_ref),
    )

    @pl.when(pl.program_id(0) == 0)
    def _():
        copies = [
            pltpu.make_async_copy(source, target, arrivals.at[i])
            for i, (source, target) in enumerate(pairs)
        ]
        for copy in copies:
            copy.start()
        for copy in copies:
            copy.wait()

    cell_count = sums_ref.shape[2]
    first_dom = pl.program_id(0) * DOM_BLOCK
    w = weights_ref[:, 0, :]
    v = velocity_ref[:, 0, :]
    particles = w.shape[1]
    wide = (4, particles)
    turned = jnp.concatenate([w[1:], w[:1]], axis=0)
    across = jnp.concatenate([w[2:], w[:2]], axis=0)
    terms = jnp.concatenate(
        [
            w * w,
            w * turned,
            w * across,
            w * jnp.broadcast_to(v[0:1], wide),
            w * jnp.broadcast_to(v[1:2], wide),
            w * jnp.broadcast_to(v[2:3], wide),
        ],
        axis=0,
    )
    high, low = split_rows(terms)
    both = jnp.concatenate([high, low], axis=0)
    owner = owner_ref[...]
    picked = []
    for d in range(DOM_BLOCK):
        named = jnp.where(owner == first_dom + d, 1.0, 0.0).astype(jnp.bfloat16)
        picked.append(both * named)
    left = jnp.concatenate(picked, axis=0)
    right = one_hot_rows(cell_ref[...], cell_count)
    sums = lax.dot_general(left, right, NT, preferred_element_type=jnp.float32)
    for d in range(DOM_BLOCK):
        at = 2 * TERMS * d
        sums_ref[d] = sums[at : at + TERMS] + sums[at + TERMS : at + 2 * TERMS]


def partial_sums(basis_weights, velocity, owner, cell_local, dom_count, cell_count):
    particles = cell_local.shape[1]
    return pl.pallas_call(
        partial_sums_kernel,
        grid=(dom_count // DOM_BLOCK,),
        in_specs=[pl.BlockSpec(memory_space=pltpu.HBM)] * 4,
        out_specs=pl.BlockSpec((DOM_BLOCK, TERMS, cell_count), lambda i: (i, 0, 0)),
        out_shape=jax.ShapeDtypeStruct((dom_count, TERMS, cell_count), jnp.float32),
        scratch_shapes=[
            pltpu.VMEM((4, 1, particles), jnp.float32),
            pltpu.VMEM((3, 1, particles), jnp.float32),
            pltpu.VMEM((1, particles), jnp.int32),
            pltpu.VMEM((1, particles), jnp.int32),
            pltpu.SemaphoreType.DMA((4,)),
        ],
        compiler_params=pltpu.CompilerParams(vmem_limit_bytes=48 * 1024 * 1024),
        name="partial_sums",
    )(*(pltpu.with_memory_space_constraint(a, pltpu.HBM) for a in (basis_weights, velocity, owner, cell_local)))


def solve_kernel(
    arrived_ref, inverse_ref, connectivity_ref,
    coefficients_ref, dom_far_ref, dom_near_ref, own_ref,
):
    cells = arrived_ref.shape[2]
    nodes = own_ref.shape[2]
    dom_odd = lax.rem(lax.axis_index("dom"), 2)
    slab_odd = lax.rem(lax.axis_index("slab"), 2)
    dom_moves = (2 * dom_odd, 2 - 2 * dom_odd, 1)
    slab_moves = (2 * slab_odd, 2 - 2 * slab_odd, 1)
    wanted = [3 * slab_move + dom_move for dom_move in dom_moves for slab_move in slab_moves]
    total = arrived_ref[0]
    for d in range(1, arrived_ref.shape[0]):
        total = total + arrived_ref[d]

    def gram(i, j):
        if i == j:
            row = i
        elif (j - i) % 4 == 1:
            row = 4 + i
        elif (i - j) % 4 == 1:
            row = 4 + j
        else:
            row = 8 + i
        return total[row : row + 1]

    wide = (4, cells)
    inverse_columns = [
        jnp.concatenate([inverse_ref[4 * i + j] for i in range(4)], axis=0) for j in range(4)
    ]
    gram_columns = [jnp.concatenate([gram(i, j) for i in range(4)], axis=0) for j in range(4)]
    solved = []
    for a in range(3):
        moment = total[12 + 4 * a : 16 + 4 * a]

        def apply(columns, vector):
            parts = [columns[j] * jnp.broadcast_to(vector[j : j + 1], wide) for j in range(4)]
            return (parts[0] + parts[1]) + (parts[2] + parts[3])

        first = apply(inverse_columns, moment)
        residual = moment - apply(gram_columns, first)
        solved.append(first + apply(inverse_columns, residual))
    coefficients_ref[...] = jnp.concatenate(
        [solved[a][i : i + 1] for i in range(4) for a in range(3)], axis=0
    )
    left, right = [], []
    for k in range(4):
        values = jnp.concatenate(
            [solved[a][k : k + 1] for a in range(3)] + [jnp.zeros((1, cells), jnp.float32)], axis=0
        )
        values = jnp.concatenate([values, values], axis=0)
        entry = connectivity_ref[k]
        move = entry // nodes
        node = entry - move * nodes
        columns = []
        upper = lax.broadcasted_iota(jnp.int32, (8, cells), 0) < 4
        for m in range(0, 10, 2):
            rows = jnp.where(upper, wanted[m], wanted[m + 1] if m < 8 else -1)
            columns.append(jnp.where(rows == move, values, 0.0))
        left.append(jnp.concatenate(columns, axis=0))
        right.append(one_hot_rows(node, nodes))
    left = jnp.concatenate(left, axis=1)
    right = jnp.concatenate(right, axis=1)
    high, low = split_rows(left)
    both = jnp.concatenate([high, low], axis=0)
    sums = lax.dot_general(both, right, NT, preferred_element_type=jnp.float32)
    sums = sums[:40] + sums[40:]
    for m in range(9):
        (dom_far_ref, dom_near_ref, own_ref)[m // 3][m % 3] = sums[4 * m : 4 * m + 4]


def solve(arrived, inverse, connectivity, node_count):
    cells = arrived.shape[2]
    return pl.pallas_call(
        solve_kernel,
        out_shape=(
            jax.ShapeDtypeStruct((12, cells), jnp.float32),
        )
        + (jax.ShapeDtypeStruct((3, 4, node_count), jnp.float32),) * 3,
        compiler_params=pltpu.CompilerParams(vmem_limit_bytes=48 * 1024 * 1024),
        name="solve",
    )(arrived, inverse, connectivity)


def swap_near(array, axis):
    devices = lax.axis_size(axis)
    return lax.ppermute(array, axis, [(i, i ^ 1) for i in range(devices)])


def swap_far_slab(array):
    slabs = lax.axis_size("slab")
    pairs = [(i, ((i + 1) ^ 1) - 1) for i in range(1, slabs - 1)]
    return lax.ppermute(array, "slab", [(0, slabs - 1)] + pairs + [(slabs - 1, 0)])


def swap_far_dom(array):
    doms, slabs = lax.axis_size("dom"), lax.axis_size("slab")
    pairs = []
    for d in range(doms):
        for s in range(slabs):
            inside = 0 < d < doms - 1
            to = (((d + 1) ^ 1) - 1) * slabs + s if inside else d * slabs + (s ^ 1)
            pairs.append((d * slabs + s, to))
    return lax.ppermute(array, ("dom", "slab"), pairs)


def per_device(basis_weights, velocity, owner_dom, cell_local, inverse, connectivity):
    particles = cell_local.shape[1]
    cells = inverse.shape[2]
    nodes = 256
    doms = lax.axis_size("dom")
    owner = owner_dom.reshape(1, particles)
    sums = partial_sums(basis_weights, velocity, owner, cell_local, doms, cells)
    arrived = lax.all_to_all(sums, "dom", split_axis=0, concat_axis=0, tiled=True)
    coefficients, dom_far, dom_near, own = solve(arrived, inverse, connectivity, nodes)
    merged = own + swap_far_dom(dom_far) + swap_near(dom_near, "dom")
    total = merged[2] + swap_near(merged[1], "slab") + swap_far_slab(merged[0])
    return coefficients.reshape(12, 1, cells), total[:3].reshape(3, 1, nodes)


def solution(mesh):
    in_specs = (
        P(None, "slab", "dom"),
        P(None, "slab", "dom"),
        P("slab", "dom", None),
        P("slab", "dom"),
        P(None, "slab", "dom"),
        P(None, "slab", "dom"),
    )
    out_specs = (P(None, "slab", "dom"), P(None, "slab", "dom"))
    return jax.shard_map(
        per_device, mesh=mesh, in_specs=in_specs, out_specs=out_specs, check_vma=False
    )
```

```python
import jax
import jax.numpy as jnp
from jax import lax
from jax.experimental import pallas as pl
from jax.experimental.pallas import tpu as pltpu
from jax.sharding import PartitionSpec as P

DOM_BLOCK = 8
TERMS = 24
SENT_BY_EVEN = (6, 0, 4, 3)
SENT_BY_ODD = (7, 1, 5, 2)
NT = (((1,), (1,)), ((), ()))


def split_rows(values):
    high = values.astype(jnp.bfloat16)
    low = (values - high.astype(jnp.float32)).astype(jnp.bfloat16)
    return high, low


def one_hot_rows(index_row, count):
    lanes = 128
    rows = lax.broadcasted_iota(jnp.int32, (count, lanes), 0).astype(jnp.bfloat16)
    index = index_row.astype(jnp.float32).astype(jnp.bfloat16)
    one, zero = jnp.bfloat16(1), jnp.bfloat16(0)
    return jnp.concatenate(
        [
            jnp.where(rows == index[:, at : at + lanes], one, zero)
            for at in range(0, index_row.shape[1], lanes)
        ],
        axis=1,
    )


def sums_by_owner(weights_ref, velocity_ref, owner_ref, cell_ref, doms, cell_count):
    w = weights_ref[:, 0, :]
    v = velocity_ref[:, 0, :]
    particles = w.shape[1]
    wide = (4, particles)
    turned = jnp.concatenate([w[1:], w[:1]], axis=0)
    across = jnp.concatenate([w[2:], w[:2]], axis=0)
    terms = jnp.concatenate(
        [
            w * w,
            w * turned,
            w * across,
            w * jnp.broadcast_to(v[0:1], wide),
            w * jnp.broadcast_to(v[1:2], wide),
            w * jnp.broadcast_to(v[2:3], wide),
        ],
        axis=0,
    )
    high, low = split_rows(terms)
    both = jnp.concatenate([high, low], axis=0)
    owner = owner_ref[...]
    picked = []
    for dom in doms:
        named = jnp.where(owner == dom, 1.0, 0.0).astype(jnp.bfloat16)
        picked.append(both * named)
    left = jnp.concatenate(picked, axis=0)
    right = one_hot_rows(cell_ref[...], cell_count)
    sums = lax.dot_general(left, right, NT, preferred_element_type=jnp.float32)
    for j in range(len(doms)):
        at = 2 * TERMS * j
        yield sums[at : at + TERMS] + sums[at + TERMS : at + 2 * TERMS]


def fetch(pairs, arrivals):
    copies = [
        pltpu.make_async_copy(source, target, arrivals.at[i])
        for i, (source, target) in enumerate(pairs)
    ]
    for copy in copies:
        copy.start()
    for copy in copies:
        copy.wait()


def few_doms_kernel(*refs):
    sources, (keep_ref, give_ref), held, arrivals = refs[:4], refs[4:6], refs[6:10], refs[10]
    fetch(list(zip(sources, held)), arrivals)
    me = lax.axis_index("dom")
    odd = lax.rem(lax.axis_index("slab"), 2)
    pairs = list(zip(SENT_BY_EVEN, SENT_BY_ODD))
    doms = [me ^ (e + odd * (o - e)) for e, o in pairs]
    doms += [me ^ (o + odd * (e - o)) for e, o in pairs]
    for k, sums in enumerate(sums_by_owner(*held, doms, keep_ref.shape[2])):
        (keep_ref, give_ref)[k // 4][k % 4] = sums


def many_doms_kernel(*refs):
    sources, sums_ref, held, arrivals = refs[:4], refs[4], refs[5:9], refs[9]

    @pl.when(pl.program_id(0) == 0)
    def _():
        fetch(list(zip(sources, held)), arrivals)

    first = pl.program_id(0) * DOM_BLOCK
    doms = [first + k for k in range(DOM_BLOCK)]
    for k, sums in enumerate(sums_by_owner(*held, doms, sums_ref.shape[2])):
        sums_ref[k] = sums


def partial_sums(arrays, dom_count, cell_count):
    few = dom_count == DOM_BLOCK
    if few:
        out_shape = [jax.ShapeDtypeStruct((4, TERMS, cell_count), jnp.float32)] * 2
        out_specs = [pl.BlockSpec((4, TERMS, cell_count), lambda i: (0, 0, 0))] * 2
    else:
        out_specs = pl.BlockSpec((DOM_BLOCK, TERMS, cell_count), lambda i: (i, 0, 0))
        out_shape = jax.ShapeDtypeStruct((dom_count, TERMS, cell_count), jnp.float32)
    return pl.pallas_call(
        few_doms_kernel if few else many_doms_kernel,
        grid=(dom_count // DOM_BLOCK,),
        in_specs=[pl.BlockSpec(memory_space=pltpu.HBM)] * len(arrays),
        out_specs=out_specs,
        out_shape=out_shape,
        scratch_shapes=[pltpu.VMEM(a.shape, a.dtype) for a in arrays]
        + [pltpu.SemaphoreType.DMA((len(arrays),))],
        compiler_params=pltpu.CompilerParams(vmem_limit_bytes=48 * 1024 * 1024),
        name="partial_sums",
    )(*(pltpu.with_memory_space_constraint(a, pltpu.HBM) for a in arrays))


def solve_kernel(*refs):
    blocks, (inverse_ref, connectivity_ref) = refs[:-6], refs[-6:-4]
    coefficients_ref, dom_far_ref, dom_near_ref, own_ref = refs[-4:]
    cells = inverse_ref.shape[2]
    nodes = own_ref.shape[2]
    dom_odd = lax.rem(lax.axis_index("dom"), 2)
    slab_odd = lax.rem(lax.axis_index("slab"), 2)
    dom_moves = (2 * dom_odd, 2 - 2 * dom_odd, 1)
    slab_moves = (2 * slab_odd, 2 - 2 * slab_odd, 1)
    wanted = [3 * slab_move + dom_move for dom_move in dom_moves for slab_move in slab_moves]
    total = sum(block[d] for block in blocks for d in range(block.shape[0]))

    def gram(i, j):
        if i == j:
            row = i
        elif (j - i) % 4 == 1:
            row = 4 + i
        elif (i - j) % 4 == 1:
            row = 4 + j
        else:
            row = 8 + i
        return total[row : row + 1]

    wide = (4, cells)
    inverse_columns = [
        jnp.concatenate([inverse_ref[4 * i + j] for i in range(4)], axis=0) for j in range(4)
    ]
    gram_columns = [jnp.concatenate([gram(i, j) for i in range(4)], axis=0) for j in range(4)]
    solved = []
    for a in range(3):
        moment = total[12 + 4 * a : 16 + 4 * a]

        def apply(columns, vector):
            parts = [columns[j] * jnp.broadcast_to(vector[j : j + 1], wide) for j in range(4)]
            return (parts[0] + parts[1]) + (parts[2] + parts[3])

        first = apply(inverse_columns, moment)
        residual = moment - apply(gram_columns, first)
        solved.append(first + apply(inverse_columns, residual))
    coefficients_ref[...] = jnp.concatenate(
        [solved[a][i : i + 1] for i in range(4) for a in range(3)], axis=0
    )
    left, right = [], []
    for k in range(4):
        values = jnp.concatenate(
            [solved[a][k : k + 1] for a in range(3)] + [jnp.zeros((1, cells), jnp.float32)], axis=0
        )
        values = jnp.concatenate([values, values], axis=0)
        entry = connectivity_ref[k]
        move = entry // nodes
        node = entry - move * nodes
        columns = []
        upper = lax.broadcasted_iota(jnp.int32, (8, cells), 0) < 4
        for m in range(0, 10, 2):
            rows = jnp.where(upper, wanted[m], wanted[m + 1] if m < 8 else -1)
            columns.append(jnp.where(rows == move, values, 0.0))
        left.append(jnp.concatenate(columns, axis=0))
        right.append(one_hot_rows(node, nodes))
    left = jnp.concatenate(left, axis=1)
    right = jnp.concatenate(right, axis=1)
    high, low = split_rows(left)
    both = jnp.concatenate([high, low], axis=0)
    sums = lax.dot_general(both, right, NT, preferred_element_type=jnp.float32)
    sums = sums[:40] + sums[40:]
    for m in range(9):
        (dom_far_ref, dom_near_ref, own_ref)[m // 3][m % 3] = sums[4 * m : 4 * m + 4]


def solve(blocks, inverse, connectivity, node_count):
    cells = inverse.shape[2]
    return pl.pallas_call(
        solve_kernel,
        out_shape=(
            jax.ShapeDtypeStruct((12, cells), jnp.float32),
        )
        + (jax.ShapeDtypeStruct((3, 4, node_count), jnp.float32),) * 3,
        compiler_params=pltpu.CompilerParams(vmem_limit_bytes=48 * 1024 * 1024),
        name="solve",
    )(*blocks, inverse, connectivity)


def send(array, dom_step, slab_step):
    doms, slabs = lax.axis_size("dom"), lax.axis_size("slab")
    pairs = []
    for d in range(doms):
        for s in range(slabs):
            to_dom, to_slab = dom_step(d, s), slab_step(s) % slabs
            if not 0 <= to_dom < doms:
                to_dom, to_slab = d, s ^ 1
            pairs.append((d * slabs + s, to_dom * slabs + to_slab))
    return lax.ppermute(array, ("dom", "slab"), pairs)


def stay(i, s=0):
    return i


def near(i, s=0):
    return i ^ 1


def far(i, s=0):
    return ((i + 1) ^ 1) - 1


def to_owners(sums):
    if not isinstance(sums, (list, tuple)):
        return [lax.all_to_all(sums, "dom", split_axis=0, concat_axis=0, tiled=True)]
    keep, give = sums
    other = send(give, stay, near)
    arrived = []
    for j in range(4):
        both = jnp.concatenate([keep[j], other[j]], axis=0)
        step = lambda d, s, j=j: d ^ (SENT_BY_ODD if s % 2 else SENT_BY_EVEN)[j]
        arrived.append(send(both, step, near))
    total = (arrived[0] + arrived[1]) + (arrived[2] + arrived[3])
    return [total[None, TERMS:], send(total[:TERMS], stay, near)[None]]


def per_device(basis_weights, velocity, owner_dom, cell_local, inverse, connectivity):
    particles = cell_local.shape[1]
    cells = inverse.shape[2]
    nodes = 256
    doms = lax.axis_size("dom")
    owner = owner_dom.reshape(1, particles)
    sums = partial_sums((basis_weights, velocity, owner, cell_local), doms, cells)
    coefficients, dom_far, dom_near, own = solve(to_owners(sums), inverse, connectivity, nodes)
    merged = own + send(dom_far, far, stay) + send(dom_near, near, stay)
    total = merged[2] + send(merged[1], stay, near) + send(merged[0], stay, far)
    return coefficients.reshape(12, 1, cells), total[:3].reshape(3, 1, nodes)


def solution(mesh):
    in_specs = (
        P(None, "slab", "dom"),
        P(None, "slab", "dom"),
        P("slab", "dom", None),
        P("slab", "dom"),
        P(None, "slab", "dom"),
        P(None, "slab", "dom"),
    )
    out_specs = (P(None, "slab", "dom"), P(None, "slab", "dom"))
    return jax.shard_map(
        per_device, mesh=mesh, in_specs=in_specs, out_specs=out_specs, check_vma=False
    )
```

```python
import jax
import jax.numpy as jnp
from jax import lax
from jax.experimental import pallas as pl
from jax.experimental.pallas import tpu as pltpu
from jax.sharding import PartitionSpec as P

DOM_BLOCK = 8
TERMS = 24
SENT_BY_EVEN = (6, 1, 4, 3)
SENT_BY_ODD = (7, 0, 5, 2)
NT = (((1,), (1,)), ((), ()))


def split_rows(values):
    high = values.astype(jnp.bfloat16)
    low = (values - high.astype(jnp.float32)).astype(jnp.bfloat16)
    return high, low


def one_hot_rows(index_row, count):
    lanes = 128
    rows = lax.broadcasted_iota(jnp.int32, (count, lanes), 0).astype(jnp.bfloat16)
    index = index_row.astype(jnp.float32).astype(jnp.bfloat16)
    one, zero = jnp.bfloat16(1), jnp.bfloat16(0)
    return jnp.concatenate(
        [
            jnp.where(rows == index[:, at : at + lanes], one, zero)
            for at in range(0, index_row.shape[1], lanes)
        ],
        axis=1,
    )


def sums_by_owner(weights_ref, velocity_ref, owner_ref, cell_ref, doms, cell_count):
    w = weights_ref[:, 0, :]
    v = velocity_ref[:, 0, :]
    particles = w.shape[1]
    wide = (4, particles)
    turned = jnp.concatenate([w[1:], w[:1]], axis=0)
    across = jnp.concatenate([w[2:], w[:2]], axis=0)
    terms = jnp.concatenate(
        [
            w * w,
            w * turned,
            w * across,
            w * jnp.broadcast_to(v[0:1], wide),
            w * jnp.broadcast_to(v[1:2], wide),
            w * jnp.broadcast_to(v[2:3], wide),
        ],
        axis=0,
    )
    high, low = split_rows(terms)
    both = jnp.concatenate([high, low], axis=0)
    owner = owner_ref[...]
    picked = []
    for dom in doms:
        named = jnp.where(owner == dom, 1.0, 0.0).astype(jnp.bfloat16)
        picked.append(both * named)
    left = jnp.concatenate(picked, axis=0)
    right = one_hot_rows(cell_ref[...], cell_count)
    sums = lax.dot_general(left, right, NT, preferred_element_type=jnp.float32)
    for j in range(len(doms)):
        at = 2 * TERMS * j
        yield sums[at : at + TERMS] + sums[at + TERMS : at + 2 * TERMS]


def fetch(pairs, arrivals):
    copies = [
        pltpu.make_async_copy(source, target, arrivals.at[i])
        for i, (source, target) in enumerate(pairs)
    ]
    for copy in copies:
        copy.start()
    for copy in copies:
        copy.wait()


def few_doms_kernel(*refs):
    sources, (keep_ref, give_ref), held, arrivals = refs[:4], refs[4:6], refs[6:10], refs[10]
    fetch(list(zip(sources, held)), arrivals)
    me = lax.axis_index("dom")
    odd = lax.rem(lax.axis_index("slab"), 2)
    pairs = list(zip(SENT_BY_EVEN, SENT_BY_ODD))
    doms = [me ^ (e + odd * (o - e)) for e, o in pairs]
    doms += [me ^ (o + odd * (e - o)) for e, o in pairs]
    for k, sums in enumerate(sums_by_owner(*held, doms, keep_ref.shape[2])):
        (keep_ref, give_ref)[k // 4][k % 4] = sums


def many_doms_kernel(*refs):
    sources, sums_ref, held, arrivals = refs[:4], refs[4], refs[5:9], refs[9]

    @pl.when(pl.program_id(0) == 0)
    def _():
        fetch(list(zip(sources, held)), arrivals)

    first = pl.program_id(0) * DOM_BLOCK
    doms = [first + k for k in range(DOM_BLOCK)]
    for k, sums in enumerate(sums_by_owner(*held, doms, sums_ref.shape[2])):
        sums_ref[k] = sums


def partial_sums(arrays, dom_count, cell_count):
    few = dom_count == DOM_BLOCK
    if few:
        out_shape = [jax.ShapeDtypeStruct((4, TERMS, cell_count), jnp.float32)] * 2
        out_specs = [pl.BlockSpec((4, TERMS, cell_count), lambda i: (0, 0, 0))] * 2
    else:
        out_specs = pl.BlockSpec((DOM_BLOCK, TERMS, cell_count), lambda i: (i, 0, 0))
        out_shape = jax.ShapeDtypeStruct((dom_count, TERMS, cell_count), jnp.float32)
    return pl.pallas_call(
        few_doms_kernel if few else many_doms_kernel,
        grid=(dom_count // DOM_BLOCK,),
        in_specs=[pl.BlockSpec(memory_space=pltpu.HBM)] * len(arrays),
        out_specs=out_specs,
        out_shape=out_shape,
        scratch_shapes=[pltpu.VMEM(a.shape, a.dtype) for a in arrays]
        + [pltpu.SemaphoreType.DMA((len(arrays),))],
        compiler_params=pltpu.CompilerParams(vmem_limit_bytes=48 * 1024 * 1024),
        name="partial_sums",
    )(*(pltpu.with_memory_space_constraint(a, pltpu.HBM) for a in arrays))


def solve_kernel(*refs):
    blocks, (inverse_ref, connectivity_ref) = refs[:-6], refs[-6:-4]
    coefficients_ref, dom_far_ref, dom_near_ref, own_ref = refs[-4:]
    cells = inverse_ref.shape[2]
    nodes = own_ref.shape[2]
    dom_odd = lax.rem(lax.axis_index("dom"), 2)
    slab_odd = lax.rem(lax.axis_index("slab"), 2)
    dom_moves = (2 * dom_odd, 2 - 2 * dom_odd, 1)
    slab_moves = (2 * slab_odd, 2 - 2 * slab_odd, 1)
    wanted = [3 * slab_move + dom_move for dom_move in dom_moves for slab_move in slab_moves]
    total = sum(block[d] for block in blocks for d in range(block.shape[0]))

    def gram(i, j):
        if i == j:
            row = i
        elif (j - i) % 4 == 1:
            row = 4 + i
        elif (i - j) % 4 == 1:
            row = 4 + j
        else:
            row = 8 + i
        return total[row : row + 1]

    wide = (4, cells)
    inverse_columns = [
        jnp.concatenate([inverse_ref[4 * i + j] for i in range(4)], axis=0) for j in range(4)
    ]
    gram_columns = [jnp.concatenate([gram(i, j) for i in range(4)], axis=0) for j in range(4)]
    solved = []
    for a in range(3):
        moment = total[12 + 4 * a : 16 + 4 * a]

        def apply(columns, vector):
            parts = [columns[j] * jnp.broadcast_to(vector[j : j + 1], wide) for j in range(4)]
            return (parts[0] + parts[1]) + (parts[2] + parts[3])

        first = apply(inverse_columns, moment)
        residual = moment - apply(gram_columns, first)
        solved.append(first + apply(inverse_columns, residual))
    coefficients_ref[...] = jnp.concatenate(
        [solved[a][i : i + 1] for i in range(4) for a in range(3)], axis=0
    )
    left, right = [], []
    for k in range(4):
        values = jnp.concatenate(
            [solved[a][k : k + 1] for a in range(3)] + [jnp.zeros((1, cells), jnp.float32)], axis=0
        )
        values = jnp.concatenate([values, values], axis=0)
        entry = connectivity_ref[k]
        move = entry // nodes
        node = entry - move * nodes
        columns = []
        upper = lax.broadcasted_iota(jnp.int32, (8, cells), 0) < 4
        for m in range(0, 10, 2):
            rows = jnp.where(upper, wanted[m], wanted[m + 1] if m < 8 else -1)
            columns.append(jnp.where(rows == move, values, 0.0))
        left.append(jnp.concatenate(columns, axis=0))
        right.append(one_hot_rows(node, nodes))
    left = jnp.concatenate(left, axis=1)
    right = jnp.concatenate(right, axis=1)
    high, low = split_rows(left)
    both = jnp.concatenate([high, low], axis=0)
    sums = lax.dot_general(both, right, NT, preferred_element_type=jnp.float32)
    sums = sums[:40] + sums[40:]
    for m in range(9):
        (dom_far_ref, dom_near_ref, own_ref)[m // 3][m % 3] = sums[4 * m : 4 * m + 4]


def solve(blocks, inverse, connectivity, node_count):
    cells = inverse.shape[2]
    return pl.pallas_call(
        solve_kernel,
        out_shape=(
            jax.ShapeDtypeStruct((12, cells), jnp.float32),
        )
        + (jax.ShapeDtypeStruct((3, 4, node_count), jnp.float32),) * 3,
        compiler_params=pltpu.CompilerParams(vmem_limit_bytes=48 * 1024 * 1024),
        name="solve",
    )(*blocks, inverse, connectivity)


def send(array, dom_step, slab_step):
    doms, slabs = lax.axis_size("dom"), lax.axis_size("slab")
    pairs = []
    for d in range(doms):
        for s in range(slabs):
            to_dom, to_slab = dom_step(d, s), slab_step(s) % slabs
            if not 0 <= to_dom < doms:
                to_dom, to_slab = d, s ^ 1
            pairs.append((d * slabs + s, to_dom * slabs + to_slab))
    return lax.ppermute(array, ("dom", "slab"), pairs)


def stay(i, s=0):
    return i


def near(i, s=0):
    return i ^ 1


def far(i, s=0):
    return ((i + 1) ^ 1) - 1


def far_of_near(i):
    return far(near(i))


def to_owners(sums):
    if not isinstance(sums, (list, tuple)):
        return [lax.all_to_all(sums, "dom", split_axis=0, concat_axis=0, tiled=True)]
    keep, give = sums
    other = send(give, stay, near)
    arrived = []
    for j in range(4):
        both = jnp.concatenate([keep[j], other[j]], axis=0)
        step = lambda d, s, j=j: d ^ (SENT_BY_ODD if s % 2 else SENT_BY_EVEN)[j]
        arrived.append(send(both, step, near))
    total = (arrived[0] + arrived[1]) + (arrived[2] + arrived[3])
    return [total[None, TERMS:], send(total[:TERMS], stay, near)[None]]


def per_device(basis_weights, velocity, owner_dom, cell_local, inverse, connectivity):
    particles = cell_local.shape[1]
    cells = inverse.shape[2]
    nodes = 256
    doms = lax.axis_size("dom")
    owner = owner_dom.reshape(1, particles)
    sums = partial_sums((basis_weights, velocity, owner, cell_local), doms, cells)
    coefficients, dom_far, dom_near, own = solve(to_owners(sums), inverse, connectivity, nodes)
    merged = send(dom_near, near, near) + send(dom_far, far, near) + send(own, stay, near)
    total = merged[1] + send(merged[2], stay, near) + send(merged[0], stay, far_of_near)
    return coefficients.reshape(12, 1, cells), total[:3].reshape(3, 1, nodes)


def solution(mesh):
    in_specs = (
        P(None, "slab", "dom"),
        P(None, "slab", "dom"),
        P("slab", "dom", None),
        P("slab", "dom"),
        P(None, "slab", "dom"),
        P(None, "slab", "dom"),
    )
    out_specs = (P(None, "slab", "dom"), P(None, "slab", "dom"))
    return jax.shard_map(
        per_device, mesh=mesh, in_specs=in_specs, out_specs=out_specs, check_vma=False
    )
```

```python
import jax
import jax.numpy as jnp
from jax import lax
from jax.experimental import pallas as pl
from jax.experimental.pallas import tpu as pltpu
from jax.sharding import PartitionSpec as P

DOM_BLOCK = 8
TERMS = 24
SENT_BY_EVEN = (6, 1, 4, 3)
SENT_BY_ODD = (7, 0, 5, 2)
NT = (((1,), (1,)), ((), ()))


def split_rows(values):
    high = values.astype(jnp.bfloat16)
    low = (values - high.astype(jnp.float32)).astype(jnp.bfloat16)
    return high, low


def one_hot_rows(index_row, count):
    lanes = 128
    rows = lax.broadcasted_iota(jnp.int32, (count, lanes), 0).astype(jnp.bfloat16)
    index = index_row.astype(jnp.float32).astype(jnp.bfloat16)
    one, zero = jnp.bfloat16(1), jnp.bfloat16(0)
    return jnp.concatenate(
        [
            jnp.where(rows == index[:, at : at + lanes], one, zero)
            for at in range(0, index_row.shape[1], lanes)
        ],
        axis=1,
    )


def sums_by_owner(weights_ref, velocity_ref, owner_ref, cell_ref, doms, cell_count):
    w = weights_ref[:, 0, :]
    v = velocity_ref[:, 0, :]
    particles = w.shape[1]
    wide = (4, particles)
    turned = jnp.concatenate([w[1:], w[:1]], axis=0)
    across = jnp.concatenate([w[2:], w[:2]], axis=0)
    terms = jnp.concatenate(
        [
            w * w,
            w * turned,
            w * across,
            w * jnp.broadcast_to(v[0:1], wide),
            w * jnp.broadcast_to(v[1:2], wide),
            w * jnp.broadcast_to(v[2:3], wide),
        ],
        axis=0,
    )
    high, low = split_rows(terms)
    both = jnp.concatenate([high, low], axis=0)
    owner = owner_ref[...]
    picked = []
    for dom in doms:
        named = jnp.where(owner == dom, 1.0, 0.0).astype(jnp.bfloat16)
        picked.append(both * named)
    left = jnp.concatenate(picked, axis=0)
    right = one_hot_rows(cell_ref[...], cell_count)
    sums = lax.dot_general(left, right, NT, preferred_element_type=jnp.float32)
    for j in range(len(doms)):
        at = 2 * TERMS * j
        yield sums[at : at + TERMS] + sums[at + TERMS : at + 2 * TERMS]


def fetch(pairs, arrivals):
    copies = [
        pltpu.make_async_copy(source, target, arrivals.at[i])
        for i, (source, target) in enumerate(pairs)
    ]
    for copy in copies:
        copy.start()
    for copy in copies:
        copy.wait()


def few_doms_kernel(*refs):
    sources, (keep_ref, give_ref), held, arrivals = refs[:4], refs[4:6], refs[6:10], refs[10]
    fetch(list(zip(sources, held)), arrivals)
    me = lax.axis_index("dom")
    odd = lax.rem(lax.axis_index("slab"), 2)
    pairs = list(zip(SENT_BY_EVEN, SENT_BY_ODD))
    doms = [me ^ (e + odd * (o - e)) for e, o in pairs]
    doms += [me ^ (o + odd * (e - o)) for e, o in pairs]
    for k, sums in enumerate(sums_by_owner(*held, doms, keep_ref.shape[2])):
        (keep_ref, give_ref)[k // 4][k % 4] = sums


def many_doms_kernel(*refs):
    sources, sums_ref, held, arrivals = refs[:4], refs[4], refs[5:9], refs[9]

    @pl.when(pl.program_id(0) == 0)
    def _():
        fetch(list(zip(sources, held)), arrivals)

    first = pl.program_id(0) * DOM_BLOCK
    doms = [first + k for k in range(DOM_BLOCK)]
    for k, sums in enumerate(sums_by_owner(*held, doms, sums_ref.shape[2])):
        sums_ref[k] = sums


def partial_sums(arrays, dom_count, cell_count):
    few = dom_count == DOM_BLOCK
    if few:
        out_shape = [jax.ShapeDtypeStruct((4, TERMS, cell_count), jnp.float32)] * 2
        out_specs = [pl.BlockSpec((4, TERMS, cell_count), lambda i: (0, 0, 0))] * 2
    else:
        out_specs = pl.BlockSpec((DOM_BLOCK, TERMS, cell_count), lambda i: (i, 0, 0))
        out_shape = jax.ShapeDtypeStruct((dom_count, TERMS, cell_count), jnp.float32)
    return pl.pallas_call(
        few_doms_kernel if few else many_doms_kernel,
        grid=(dom_count // DOM_BLOCK,),
        in_specs=[pl.BlockSpec(memory_space=pltpu.HBM)] * len(arrays),
        out_specs=out_specs,
        out_shape=out_shape,
        scratch_shapes=[pltpu.VMEM(a.shape, a.dtype) for a in arrays]
        + [pltpu.SemaphoreType.DMA((len(arrays),))],
        compiler_params=pltpu.CompilerParams(vmem_limit_bytes=48 * 1024 * 1024),
        name="partial_sums",
    )(*(pltpu.with_memory_space_constraint(a, pltpu.HBM) for a in arrays))


def solve_kernel(*refs):
    blocks, (inverse_ref, connectivity_ref) = refs[:-6], refs[-6:-4]
    coefficients_ref, dom_far_ref, dom_near_ref, own_ref = refs[-4:]
    cells = inverse_ref.shape[2]
    nodes = own_ref.shape[2]
    dom_odd = lax.rem(lax.axis_index("dom"), 2)
    slab_odd = lax.rem(lax.axis_index("slab"), 2)
    dom_moves = (2 * dom_odd, 2 - 2 * dom_odd, 1)
    slab_moves = (2 * slab_odd, 2 - 2 * slab_odd, 1)
    wanted = [3 * slab_move + dom_move for dom_move in dom_moves for slab_move in slab_moves]
    total = sum(block[d] for block in blocks for d in range(block.shape[0]))

    def gram(i, j):
        if i == j:
            row = i
        elif (j - i) % 4 == 1:
            row = 4 + i
        elif (i - j) % 4 == 1:
            row = 4 + j
        else:
            row = 8 + i
        return total[row : row + 1]

    wide = (4, cells)
    inverse_columns = [
        jnp.concatenate([inverse_ref[4 * i + j] for i in range(4)], axis=0) for j in range(4)
    ]
    gram_columns = [jnp.concatenate([gram(i, j) for i in range(4)], axis=0) for j in range(4)]
    solved = []
    for a in range(3):
        moment = total[12 + 4 * a : 16 + 4 * a]

        def apply(columns, vector):
            parts = [columns[j] * jnp.broadcast_to(vector[j : j + 1], wide) for j in range(4)]
            return (parts[0] + parts[1]) + (parts[2] + parts[3])

        first = apply(inverse_columns, moment)
        residual = moment - apply(gram_columns, first)
        solved.append(first + apply(inverse_columns, residual))
    coefficients_ref[...] = jnp.concatenate(
        [solved[a][i : i + 1] for i in range(4) for a in range(3)], axis=0
    )
    left, right = [], []
    for k in range(4):
        values = jnp.concatenate(
            [solved[a][k : k + 1] for a in range(3)] + [jnp.zeros((1, cells), jnp.float32)], axis=0
        )
        values = jnp.concatenate([values, values], axis=0)
        entry = connectivity_ref[k]
        move = entry // nodes
        node = entry - move * nodes
        columns = []
        upper = lax.broadcasted_iota(jnp.int32, (8, cells), 0) < 4
        for m in range(0, 10, 2):
            rows = jnp.where(upper, wanted[m], wanted[m + 1] if m < 8 else -1)
            columns.append(jnp.where(rows == move, values, 0.0))
        left.append(jnp.concatenate(columns, axis=0))
        right.append(one_hot_rows(node, nodes))
    left = jnp.concatenate(left, axis=1)
    right = jnp.concatenate(right, axis=1)
    high, low = split_rows(left)
    both = jnp.concatenate([high, low], axis=0)
    sums = lax.dot_general(both, right, NT, preferred_element_type=jnp.float32)
    sums = sums[:40] + sums[40:]
    for m in range(9):
        (dom_far_ref, dom_near_ref, own_ref)[m // 3][m % 3] = sums[4 * m : 4 * m + 4]


def solve(blocks, inverse, connectivity, node_count):
    cells = inverse.shape[2]
    return pl.pallas_call(
        solve_kernel,
        out_shape=(
            jax.ShapeDtypeStruct((12, cells), jnp.float32),
        )
        + (jax.ShapeDtypeStruct((3, 4, node_count), jnp.float32),) * 3,
        compiler_params=pltpu.CompilerParams(vmem_limit_bytes=48 * 1024 * 1024),
        name="solve",
    )(*blocks, inverse, connectivity)


def send(array, dom_step, slab_step):
    doms, slabs = lax.axis_size("dom"), lax.axis_size("slab")
    pairs = []
    for d in range(doms):
        for s in range(slabs):
            to_dom, to_slab = dom_step(d, s), slab_step(s) % slabs
            if not 0 <= to_dom < doms:
                to_dom, to_slab = d, s ^ 1
            pairs.append((d * slabs + s, to_dom * slabs + to_slab))
    return lax.ppermute(array, ("dom", "slab"), pairs)


def stay(i, s=0):
    return i


def near(i, s=0):
    return i ^ 1


def far(i, s=0):
    return ((i + 1) ^ 1) - 1


def far_of_near(i):
    return far(near(i))


def to_owners(sums):
    if not isinstance(sums, (list, tuple)):
        return [lax.all_to_all(sums, "dom", split_axis=0, concat_axis=0, tiled=True)]
    keep, give = sums
    other = [*send(give[:1], stay, near), *send(give[1:], stay, near)]
    arrived = []
    for j in range(4):
        both = jnp.concatenate([keep[j], other[j]], axis=0)
        step = lambda d, s, j=j: d ^ (SENT_BY_ODD if s % 2 else SENT_BY_EVEN)[j]
        arrived.append(send(both, step, near))
    total = (arrived[0] + arrived[1]) + (arrived[2] + arrived[3])
    return [total[None, TERMS:], send(total[:TERMS], stay, near)[None]]


def per_device(basis_weights, velocity, owner_dom, cell_local, inverse, connectivity):
    particles = cell_local.shape[1]
    cells = inverse.shape[2]
    nodes = 256
    doms = lax.axis_size("dom")
    owner = owner_dom.reshape(1, particles)
    sums = partial_sums((basis_weights, velocity, owner, cell_local), doms, cells)
    coefficients, dom_far, dom_near, own = solve(to_owners(sums), inverse, connectivity, nodes)
    merged = send(dom_near, near, near) + send(dom_far, far, near) + send(own, stay, near)
    total = merged[1] + send(merged[2], stay, near) + send(merged[0], stay, far_of_near)
    return coefficients.reshape(12, 1, cells), total[:3].reshape(3, 1, nodes)


def solution(mesh):
    in_specs = (
        P(None, "slab", "dom"),
        P(None, "slab", "dom"),
        P("slab", "dom", None),
        P("slab", "dom"),
        P(None, "slab", "dom"),
        P(None, "slab", "dom"),
    )
    out_specs = (P(None, "slab", "dom"), P(None, "slab", "dom"))
    return jax.shard_map(
        per_device, mesh=mesh, in_specs=in_specs, out_specs=out_specs, check_vma=False
    )
```
